512 devices in a mesh: items: 8 (over y), codes: 64 (over x, z, core).
Axes of the slice: x: 4, y: 8, z: 8, core: 2. Of those that a mesh axis runs over, the one named last changes fastest.
Arguments:
- residuals: bfloat16 [8192, 256], P(('items', 'codes')), may hold values from -6 to 6
- codebook: bfloat16 [16384, 256], P('codes'), may hold values from -6 to 6
Outputs:
- new_codebook: float32 [16384, 256], P('codes')
- next_residuals: float32 [8192, 256], P(('items', 'codes'))
The draws below stay inside these ranges and needn't reach their ends.
All inputs are finite; a program needn't handle non-finite values.
Results may differ from the reference program's by a relative error of at most 0.0024.
Values may be sent and summed in bfloat16 or wider, within the bound.
No kernel may reach another device: no remote copies, remote signals or barrier semaphores. Data moves between devices by JAX's collectives and lax.ppermute only.
A program may use at most 64 MiB of HBM per device.

```python
import jax
import jax.numpy as jnp
from jax import lax

D = 256
ITERS = 3
CODES = 16384
ITEMS = 8192


def block_scale(key, extent, pieces, smallest, top_value):
    def one(position, shards_of):
        heights = jax.random.uniform(jax.random.fold_in(jax.random.fold_in(key, 6), position), (shards_of,), jnp.float32, smallest / len(pieces), top_value / len(pieces))
        return jnp.repeat(jnp.exp(heights), extent[position] // shards_of).reshape((-1,) + (1,) * (len(extent) - position - 1))

    loudness = one(*pieces[0])
    for cut in pieces[1:]:
        loudness = loudness * one(*cut)
    return loudness


def bell_draw(stream_key, shape, scale, limit, split=(), dtype=jnp.bfloat16):
    array = jax.random.normal(stream_key, shape, jnp.float32) * scale
    if len(split) > 0:
        array = block_scale(stream_key, shape, split, -0.22, 0.18) * array
    return jnp.clip(array, min=-limit, max=limit).astype(dtype)


def setup_inputs(seed: int = 0) -> dict:
    keys = jax.random.split(jax.random.key(seed), 3)
    return {
        "residuals": bell_draw(keys[0], (ITEMS, D), 1.0, 6.0, ((0, 512),)),
        "codebook": bell_draw(keys[1], (CODES, D), 1.0, 6.0, ((0, 64),)),
    }


EPSILON = 1e-06
SHARPNESS = 40.0

def reference(residuals, codebook):
    items_total = residuals.shape[0]
    codes_total = codebook.shape[0]
    feature_count = residuals.shape[1]
    rows_float = residuals.astype(jnp.float32)
    codes_float = codebook.astype(jnp.float32)
    row_scale = lax.rsqrt(lax.optimization_barrier(jnp.mean(rows_float * rows_float, axis=1)) + EPSILON)
    code_scale = lax.rsqrt(lax.optimization_barrier(jnp.mean(codes_float * codes_float, axis=1)) + EPSILON)
    block_rows = min(4096, items_total)
    block_count = items_total // block_rows
    row_blocks = residuals.reshape(block_count, block_rows, feature_count)
    scale_blocks = row_scale.reshape(block_count, block_rows)

    def kernel_block(inputs):
        block, scales = inputs
        similarity = lax.dot_general(block, codebook, (((1,), (1,)), ((), ())), preferred_element_type=jnp.float32)
        return jnp.exp(SHARPNESS * similarity * scales[:, None] * code_scale[None, :] / feature_count)
    kernel = lax.map(kernel_block, (row_blocks, scale_blocks))
    balance = items_total / codes_total
    weights_rows = jnp.ones((block_count, block_rows), jnp.float32)
    weights_cols = jnp.ones((codes_total,), jnp.float32)
    for sweep in range(ITERS):
        column_total = jnp.einsum('bn,bnk->k', weights_rows, kernel, precision=lax.Precision.HIGHEST)
        weights_cols = balance / column_total
        row_total = jnp.einsum('bnk,k->bn', kernel, weights_cols, precision=lax.Precision.HIGHEST)
        weights_rows = 1.0 / row_total

    def finish(totals, inputs):
        kernel_rows, row_weights, block = inputs
        numerator, mass = totals
        transport = (kernel_rows * row_weights[:, None] * weights_cols[None, :]).astype(jnp.bfloat16)
        numerator = numerator + lax.dot_general(transport, block, (((0,), (0,)), ((), ())), preferred_element_type=jnp.float32)
        mass = mass + lax.optimization_barrier(jnp.sum(transport.astype(jnp.float32), axis=0))
        rebuilt = jnp.dot(transport, codebook, preferred_element_type=jnp.float32)
        return ((numerator, mass), block.astype(jnp.float32) - rebuilt)
    start_totals = (jnp.zeros((codes_total, feature_count), jnp.float32), jnp.zeros((codes_total,), jnp.float32))
    (numerator, mass), following = lax.scan(finish, start_totals, (kernel, weights_rows, row_blocks))
    return (numerator / mass[:, None], following.reshape(items_total, feature_count))
```

```python
import jax
import jax.numpy as jnp
from jax import lax
from jax.sharding import Mesh, PartitionSpec as P

ITERS = 3
EPSILON = 1e-06
SHARPNESS = 40.0

ITEM_AXES = ("y",)
CODE_AXES = ("x", "z", "c")


def spread(block, axes):
    members = lax.axis_size(axes)
    copies = jnp.broadcast_to(block[None], (members,) + block.shape)
    return lax.all_to_all(copies, axes, 0, 0, tiled=True)


def shards(residuals, codebook):
    rows, width = residuals.shape
    codes = codebook.shape[0]
    groups = lax.axis_size(ITEM_AXES)
    parts = lax.axis_size(CODE_AXES)
    gathered = spread(residuals, CODE_AXES).reshape(parts * rows, width)
    rows_float = gathered.astype(jnp.float32)
    codes_float = codebook.astype(jnp.float32)
    row_scale = lax.rsqrt(jnp.mean(rows_float * rows_float, axis=1) + EPSILON)
    code_scale = lax.rsqrt(jnp.mean(codes_float * codes_float, axis=1) + EPSILON)
    similarity = lax.dot_general(
        gathered, codebook, (((1,), (1,)), ((), ())), preferred_element_type=jnp.float32
    )
    kernel = jnp.exp(
        SHARPNESS * similarity * row_scale[:, None] * code_scale[None, :] / width
    )
    balance = (gathered.shape[0] * groups) / (codes * parts)
    weights_rows = None
    for sweep in range(ITERS):
        scaled = kernel if weights_rows is None else kernel * weights_rows[:, None]
        column_total = jnp.sum(spread(jnp.sum(scaled, axis=0), ITEM_AXES), axis=0)
        weights_cols = balance / column_total
        row_part = jnp.sum(kernel * weights_cols[None, :], axis=1)
        row_total = jnp.sum(spread(row_part, CODE_AXES), axis=0)
        weights_rows = 1.0 / row_total
    shares = (kernel * weights_cols[None, :]).astype(jnp.bfloat16)
    rebuilt = jnp.dot(shares, codebook, preferred_element_type=jnp.float32)
    rebuilt = rebuilt.astype(jnp.bfloat16).reshape(parts, rows, width)
    rebuilt = lax.all_to_all(rebuilt, CODE_AXES, 0, 0, tiled=True)
    rebuilt = jnp.sum(rebuilt.astype(jnp.float32), axis=0)

    transport = (kernel * weights_rows[:, None] * weights_cols[None, :]).astype(jnp.bfloat16)
    numerator = lax.dot_general(
        transport, gathered, (((0,), (0,)), ((), ())), preferred_element_type=jnp.float32
    )
    mass = jnp.sum(transport.astype(jnp.float32), axis=0)
    share = codes // groups
    high = mass.astype(jnp.bfloat16)
    low = (mass - high.astype(jnp.float32)).astype(jnp.bfloat16)
    masses = jnp.stack([high.reshape(groups, share), low.reshape(groups, share)], axis=1)
    masses = jnp.pad(masses, ((0, 0), (0, 14), (0, width - share)))
    packed = jnp.concatenate(
        [numerator.astype(jnp.bfloat16).reshape(groups, share, width), masses], axis=1
    )
    packed = lax.all_to_all(packed, ITEM_AXES, 0, 0, tiled=True)
    total = jnp.sum(packed.astype(jnp.float32), axis=0)
    mass_total = total[share, :share] + total[share + 1, :share]
    means = (total[:share] / mass_total[:, None]).astype(jnp.bfloat16)
    new_codebook = spread(means, ITEM_AXES).reshape(codes, width).astype(jnp.float32)

    mine = lax.axis_index(CODE_AXES) * rows
    own = lax.dynamic_slice_in_dim(weights_rows, mine, rows)
    following = residuals.astype(jnp.float32) - rebuilt * own[:, None]
    return (new_codebook, following)


def solution(mesh):
    fine = Mesh(mesh.devices.reshape(8, 4, 8, 2), ("y", "x", "z", "c"))
    return jax.shard_map(
        shards,
        mesh=fine,
        in_specs=(P(("y", "x", "z", "c"), None), P(("x", "z", "c"), None)),
        out_specs=(P(("x", "z", "c"), None), P(("y", "x", "z", "c"), None)),
        check_vma=False,
    )
```

```python
import jax
import jax.numpy as jnp
from jax import lax
from jax.sharding import Mesh, PartitionSpec as P

ITERS = 3
EPSILON = 1e-06
SHARPNESS = 40.0

ITEM_AXES = ("c", "y")
CODE_AXES = ("x", "z")


def spread(block, axes):
    members = lax.axis_size(axes)
    copies = jnp.broadcast_to(block[None], (members,) + block.shape)
    return lax.all_to_all(copies, axes, 0, 0, tiled=True)


def shards(residuals, codebook):
    rows, width = residuals.shape
    items = rows * lax.axis_size(CODE_AXES)
    codes = codebook.shape[0] * lax.axis_size("c")
    groups = lax.axis_size(ITEM_AXES)
    parts = lax.axis_size(CODE_AXES)
    codebook = spread(codebook, "c").reshape(codes, width)
    gathered = spread(residuals, CODE_AXES).reshape(items, width)
    rows_float = gathered.astype(jnp.float32)
    codes_float = codebook.astype(jnp.float32)
    row_scale = lax.rsqrt(jnp.mean(rows_float * rows_float, axis=1) + EPSILON)
    code_scale = lax.rsqrt(jnp.mean(codes_float * codes_float, axis=1) + EPSILON)
    similarity = lax.dot_general(
        gathered, codebook, (((1,), (1,)), ((), ())), preferred_element_type=jnp.float32
    )
    kernel = jnp.exp(
        SHARPNESS * similarity * row_scale[:, None] * code_scale[None, :] / width
    )
    balance = (items * groups) / (codes * parts)
    weights_rows = None
    for _ in range(ITERS):
        scaled = kernel if weights_rows is None else kernel * weights_rows[:, None]
        column_total = jnp.sum(spread(jnp.sum(scaled, axis=0), ITEM_AXES), axis=0)
        weights_cols = balance / column_total
        row_part = jnp.sum(kernel * weights_cols[None, :], axis=1)
        row_total = jnp.sum(spread(row_part, CODE_AXES), axis=0)
        weights_rows = 1.0 / row_total

    transport = (
        kernel * weights_rows[:, None] * weights_cols[None, :]
    ).astype(jnp.bfloat16)
    numerator = lax.dot_general(
        transport, gathered, (((0,), (0,)), ((), ())), preferred_element_type=jnp.float32
    )
    mass = jnp.sum(transport.astype(jnp.float32), axis=0)
    share = codes // groups
    high = mass.astype(jnp.bfloat16)
    low = (mass - high.astype(jnp.float32)).astype(jnp.bfloat16)
    masses = jnp.stack([high.reshape(groups, share), low.reshape(groups, share)], axis=1)
    masses = jnp.pad(masses, ((0, 0), (0, 6), (0, width - share)))
    packed = jnp.concatenate(
        [numerator.astype(jnp.bfloat16).reshape(groups, share, width), masses], axis=1
    )
    packed = lax.all_to_all(packed, ITEM_AXES, 0, 0, tiled=True)

    shares = (kernel * weights_cols[None, :]).astype(jnp.bfloat16)
    rebuilt = jnp.dot(shares, codebook, preferred_element_type=jnp.float32)
    rebuilt = rebuilt.astype(jnp.bfloat16).reshape(parts, rows, width)
    rebuilt = lax.all_to_all(rebuilt, CODE_AXES, 0, 0, tiled=True)

    total = jnp.sum(packed.astype(jnp.float32), axis=0)
    mass_total = total[share, :share] + total[share + 1, :share]
    means = total[:share] / mass_total[:, None]
    new_codebook = spread(means, "y").reshape(-1, width)

    rebuilt = jnp.sum(rebuilt.astype(jnp.float32), axis=0)
    mine = lax.axis_index(CODE_AXES) * rows
    own = lax.dynamic_slice_in_dim(weights_rows, mine, rows)
    following = residuals.astype(jnp.float32) - rebuilt * own[:, None]
    return (new_codebook, following)


def solution(mesh):
    fine = Mesh(mesh.devices.reshape(8, 4, 8, 2), ("y", "x", "z", "c"))
    return jax.shard_map(
        shards,
        mesh=fine,
        in_specs=(P(("y", "x", "z", "c"), None), P(("x", "z", "c"), None)),
        out_specs=(P(("x", "z", "c"), None), P(("y", "x", "z", "c"), None)),
        check_vma=False,
    )
```

```python
import jax
import jax.numpy as jnp
from jax import lax
from jax.sharding import Mesh, PartitionSpec as P

ITERS = 3
EPSILON = 1e-06
SHARPNESS = 40.0

ITEM_AXES = ("c", "y")
CODE_AXES = ("x", "z")


def spread(block, axes):
    members = lax.axis_size(axes)
    copies = jnp.broadcast_to(block[None], (members,) + block.shape)
    return lax.all_to_all(copies, axes, 0, 0, tiled=True)


def shards(residuals, codebook):
    rows, width = residuals.shape
    items = rows * lax.axis_size(CODE_AXES)
    codes = codebook.shape[0] * lax.axis_size("c")
    groups = lax.axis_size(ITEM_AXES)
    parts = lax.axis_size(CODE_AXES)
    gathered = spread(residuals, CODE_AXES).reshape(items, width)
    other = lax.ppermute(codebook, "c", [(0, 1), (1, 0)])
    first = lax.axis_index("c") == 0
    codebook = jnp.concatenate(
        [jnp.where(first, codebook, other), jnp.where(first, other, codebook)]
    )
    codes_float = codebook.astype(jnp.float32)
    code_scale = lax.rsqrt(jnp.mean(codes_float * codes_float, axis=1) + EPSILON)
    rows_float = gathered.astype(jnp.float32)
    row_scale = lax.rsqrt(jnp.mean(rows_float * rows_float, axis=1) + EPSILON)
    similarity = lax.dot_general(
        gathered, codebook, (((1,), (1,)), ((), ())), preferred_element_type=jnp.float32
    )
    kernel = jnp.exp(
        SHARPNESS * similarity * row_scale[:, None] * code_scale[None, :] / width
    )
    balance = (items * groups) / (codes * parts)
    weights_rows = None
    for _ in range(ITERS):
        scaled = kernel if weights_rows is None else kernel * weights_rows[:, None]
        column_total = jnp.sum(spread(jnp.sum(scaled, axis=0), ITEM_AXES), axis=0)
        weights_cols = balance / column_total
        row_part = jnp.sum(kernel * weights_cols[None, :], axis=1)
        row_total = jnp.sum(spread(row_part, CODE_AXES), axis=0)
        weights_rows = 1.0 / row_total

    transport = (
        kernel * weights_rows[:, None] * weights_cols[None, :]
    ).astype(jnp.bfloat16)
    numerator = lax.dot_general(
        transport, gathered, (((0,), (0,)), ((), ())), preferred_element_type=jnp.float32
    )
    mass = jnp.sum(transport.astype(jnp.float32), axis=0)
    share = codes // groups
    high = mass.astype(jnp.bfloat16)
    low = (mass - high.astype(jnp.float32)).astype(jnp.bfloat16)
    masses = jnp.stack([high.reshape(groups, share), low.reshape(groups, share)], axis=1)
    masses = jnp.pad(masses, ((0, 0), (0, 6), (0, width - share)))
    packed = jnp.concatenate(
        [numerator.astype(jnp.bfloat16).reshape(groups, share, width), masses], axis=1
    )
    packed = lax.all_to_all(packed, ITEM_AXES, 0, 0, tiled=True)

    shares = (kernel * weights_cols[None, :]).astype(jnp.bfloat16)
    rebuilt = jnp.dot(shares, codebook, preferred_element_type=jnp.float32)
    rebuilt = rebuilt.astype(jnp.bfloat16).reshape(parts, rows, width)
    rebuilt = lax.all_to_all(rebuilt, CODE_AXES, 0, 0, tiled=True)

    total = jnp.sum(packed.astype(jnp.float32), axis=0)
    mass_total = total[share, :share] + total[share + 1, :share]
    means = total[:share] / mass_total[:, None]
    new_codebook = lax.all_gather(means, "y", axis=0, tiled=True)

    rebuilt = jnp.sum(rebuilt.astype(jnp.float32), axis=0)
    mine = lax.axis_index(CODE_AXES) * rows
    own = lax.dynamic_slice_in_dim(weights_rows, mine, rows)
    following = residuals.astype(jnp.float32) - rebuilt * own[:, None]
    return (new_codebook, following)


def solution(mesh):
    fine = Mesh(mesh.devices.reshape(8, 4, 8, 2), ("y", "x", "z", "c"))
    return jax.shard_map(
        shards,
        mesh=fine,
        in_specs=(P(("y", "x", "z", "c"), None), P(("x", "z", "c"), None)),
        out_specs=(P(("x", "z", "c"), None), P(("y", "x", "z", "c"), None)),
        check_vma=False,
    )
```

```python
import jax
import jax.numpy as jnp
from jax import lax
from jax.sharding import Mesh, PartitionSpec as P

ITERS = 3
EPSILON = 1e-06
SHARPNESS = 40.0
MEANS = jnp.float16

ITEM_AXES = ("c", "y")
CODE_AXES = ("x", "z")


def spread(block, axes):
    members = lax.axis_size(axes)
    copies = jnp.broadcast_to(block[None], (members,) + block.shape)
    return lax.all_to_all(copies, axes, 0, 0, tiled=True)


def two_terms(values):
    high = values.astype(jnp.bfloat16)
    return high, (values - high.astype(jnp.float32)).astype(jnp.bfloat16)


def shards(residuals, codebook):
    rows, width = residuals.shape
    items = rows * lax.axis_size(CODE_AXES)
    codes = codebook.shape[0] * lax.axis_size("c")
    groups = lax.axis_size(ITEM_AXES)
    parts = lax.axis_size(CODE_AXES)
    gathered = spread(residuals, CODE_AXES).reshape(items, width)
    other = lax.ppermute(codebook, "c", [(0, 1), (1, 0)])
    first = lax.axis_index("c") == 0
    codebook = jnp.concatenate(
        [jnp.where(first, codebook, other), jnp.where(first, other, codebook)]
    )
    codes_float = codebook.astype(jnp.float32)
    code_scale = lax.rsqrt(jnp.mean(codes_float * codes_float, axis=1) + EPSILON)
    rows_float = gathered.astype(jnp.float32)
    row_scale = lax.rsqrt(jnp.mean(rows_float * rows_float, axis=1) + EPSILON)
    similarity = lax.dot_general(
        gathered, codebook, (((1,), (1,)), ((), ())), preferred_element_type=jnp.float32
    )
    kernel = jnp.exp(
        SHARPNESS * similarity * row_scale[:, None] * code_scale[None, :] / width
    )
    balance = (items * groups) / (codes * parts)
    weights_rows = None
    for sweep in range(ITERS):
        scaled = kernel if weights_rows is None else kernel * weights_rows[:, None]
        column_total = jnp.sum(spread(jnp.sum(scaled, axis=0), ITEM_AXES), axis=0)
        weights_cols = balance / column_total
        row_part = jnp.sum(kernel * weights_cols[None, :], axis=1)
        if sweep < ITERS - 1:
            row_total = jnp.sum(spread(row_part, CODE_AXES), axis=0)
            weights_rows = 1.0 / row_total

    shares = (kernel * weights_cols[None, :]).astype(jnp.bfloat16)
    products = jnp.dot(shares, codebook, preferred_element_type=jnp.float32)
    products = products.astype(jnp.bfloat16).reshape(parts, rows, width)
    terms = jnp.concatenate([t.reshape(-1, width) for t in two_terms(row_part)])
    extra = terms.shape[0]
    terms = jnp.pad(terms, ((0, -extra % 8), (0, 0)))
    terms = jnp.broadcast_to(terms[None], (parts,) + terms.shape)
    packed = jnp.concatenate([products, terms], axis=1)
    packed = lax.all_to_all(packed, CODE_AXES, 0, 0, tiled=True)
    total = jnp.sum(packed.astype(jnp.float32), axis=0)
    middle = rows + extra // 2
    row_total = total[rows:middle] + total[middle : rows + extra]
    weights_rows = 1.0 / row_total.reshape(items)

    transport = (
        kernel * weights_rows[:, None] * weights_cols[None, :]
    ).astype(jnp.bfloat16)
    numerator = lax.dot_general(
        transport, gathered, (((0,), (0,)), ((), ())), preferred_element_type=jnp.float32
    )
    mass = jnp.sum(transport.astype(jnp.float32), axis=0)
    share = codes // groups
    masses = jnp.stack([t.reshape(groups, share) for t in two_terms(mass)], axis=1)
    masses = jnp.pad(masses, ((0, 0), (0, 6), (0, width - share)))
    packed = jnp.concatenate(
        [numerator.astype(jnp.bfloat16).reshape(groups, share, width), masses], axis=1
    )
    packed = lax.all_to_all(packed, ITEM_AXES, 0, 0, tiled=True)

    mine = lax.axis_index(CODE_AXES) * rows
    own = lax.dynamic_slice_in_dim(weights_rows, mine, rows)
    following = residuals.astype(jnp.float32) - total[:rows] * own[:, None]

    total = jnp.sum(packed.astype(jnp.float32), axis=0)
    mass_total = total[share, :share] + total[share + 1, :share]
    means = total[:share] / mass_total[:, None]
    new_codebook = spread(means.astype(MEANS), "y").reshape(-1, width)
    new_codebook = new_codebook.astype(jnp.float32)
    return (new_codebook, following)


def solution(mesh):
    fine = Mesh(mesh.devices.reshape(8, 4, 8, 2), ("y", "x", "z", "c"))
    return jax.shard_map(
        shards,
        mesh=fine,
        in_specs=(P(("y", "x", "z", "c"), None), P(("x", "z", "c"), None)),
        out_specs=(P(("x", "z", "c"), None), P(("y", "x", "z", "c"), None)),
        check_vma=False,
    )
```

```python
import jax
import jax.numpy as jnp
from jax import lax
from jax.sharding import Mesh, PartitionSpec as P

ITERS = 3
EPSILON = 1e-06
SHARPNESS = 40.0
MEANS = jnp.float16

ITEM_AXES = ("c", "y")
CODE_AXES = ("x", "z")


def spread(block, axes):
    members = lax.axis_size(axes)
    copies = jnp.broadcast_to(block[None], (members,) + block.shape)
    return lax.all_to_all(copies, axes, 0, 0, tiled=True)


def total_over(part, axes):
    lanes = 256
    parts = spread(part.astype(jnp.bfloat16).reshape(-1, lanes), axes)
    return jnp.sum(parts.astype(jnp.float32), axis=0).reshape(part.shape)


def two_terms(values):
    high = values.astype(jnp.bfloat16)
    return high, (values - high.astype(jnp.float32)).astype(jnp.bfloat16)


def shards(residuals, codebook):
    rows, width = residuals.shape
    items = rows * lax.axis_size(CODE_AXES)
    codes = codebook.shape[0] * lax.axis_size("c")
    groups = lax.axis_size(ITEM_AXES)
    parts = lax.axis_size(CODE_AXES)
    gathered = spread(residuals, CODE_AXES).reshape(items, width)
    other = lax.ppermute(codebook, "c", [(0, 1), (1, 0)])
    first = lax.axis_index("c") == 0
    codebook = jnp.concatenate(
        [jnp.where(first, codebook, other), jnp.where(first, other, codebook)]
    )
    codes_float = codebook.astype(jnp.float32)
    code_scale = lax.rsqrt(jnp.mean(codes_float * codes_float, axis=1) + EPSILON)
    rows_float = gathered.astype(jnp.float32)
    row_scale = lax.rsqrt(jnp.mean(rows_float * rows_float, axis=1) + EPSILON)
    similarity = lax.dot_general(
        gathered, codebook, (((1,), (1,)), ((), ())), preferred_element_type=jnp.float32
    )
    kernel = jnp.exp(
        SHARPNESS * similarity * row_scale[:, None] * code_scale[None, :] / width
    )
    balance = (items * groups) / (codes * parts)
    weights_rows = None
    for sweep in range(ITERS):
        scaled = kernel if weights_rows is None else kernel * weights_rows[:, None]
        column_total = total_over(jnp.sum(scaled, axis=0), ITEM_AXES)
        weights_cols = balance / column_total
        row_part = jnp.sum(kernel * weights_cols[None, :], axis=1)
        if sweep < ITERS - 1:
            row_total = total_over(row_part, CODE_AXES)
            weights_rows = 1.0 / row_total

    shares = (kernel * weights_cols[None, :]).astype(jnp.bfloat16)
    products = jnp.dot(shares, codebook, preferred_element_type=jnp.float32)
    products = products.astype(jnp.bfloat16).reshape(parts, rows, width)
    terms = jnp.concatenate([t.reshape(-1, width) for t in two_terms(row_part)])
    extra = terms.shape[0]
    terms = jnp.pad(terms, ((0, -extra % 8), (0, 0)))
    terms = jnp.broadcast_to(terms[None], (parts,) + terms.shape)
    packed = jnp.concatenate([products, terms], axis=1)
    packed = lax.all_to_all(packed, CODE_AXES, 0, 0, tiled=True)
    total = jnp.sum(packed.astype(jnp.float32), axis=0)
    middle = rows + extra // 2
    row_total = total[rows:middle] + total[middle : rows + extra]
    weights_rows = 1.0 / row_total.reshape(items)

    transport = (
        kernel * weights_rows[:, None] * weights_cols[None, :]
    ).astype(jnp.bfloat16)
    numerator = lax.dot_general(
        transport, gathered, (((0,), (0,)), ((), ())), preferred_element_type=jnp.float32
    )
    mass = jnp.sum(transport.astype(jnp.float32), axis=0)
    share = codes // groups
    masses = jnp.stack([t.reshape(groups, share) for t in two_terms(mass)], axis=1)
    masses = jnp.pad(masses, ((0, 0), (0, 6), (0, width - share)))
    packed = jnp.concatenate(
        [numerator.astype(jnp.bfloat16).reshape(groups, share, width), masses], axis=1
    )
    packed = lax.all_to_all(packed, ITEM_AXES, 0, 0, tiled=True)

    mine = lax.axis_index(CODE_AXES) * rows
    own = lax.dynamic_slice_in_dim(weights_rows, mine, rows)
    following = residuals.astype(jnp.float32) - total[:rows] * own[:, None]

    total = jnp.sum(packed.astype(jnp.float32), axis=0)
    mass_total = total[share, :share] + total[share + 1, :share]
    means = total[:share] / mass_total[:, None]
    new_codebook = spread(means.astype(MEANS), "y").reshape(-1, width)
    new_codebook = new_codebook.astype(jnp.float32)
    return (new_codebook, following)


def solution(mesh):
    fine = Mesh(mesh.devices.reshape(8, 4, 8, 2), ("y", "x", "z", "c"))
    return jax.shard_map(
        shards,
        mesh=fine,
        in_specs=(P(("y", "x", "z", "c"), None), P(("x", "z", "c"), None)),
        out_specs=(P(("x", "z", "c"), None), P(("y", "x", "z", "c"), None)),
        check_vma=False,
    )
```

```python
import jax
import jax.numpy as jnp
from jax import lax
from jax.sharding import Mesh, PartitionSpec as P

ITERS = 3
EPSILON = 1e-06
SHARPNESS = 40.0
MEANS = jnp.float16

ITEM_AXES = ("x", "c", "l")


def spread(block, axes):
    members = lax.axis_size(axes)
    copies = jnp.broadcast_to(block[None], (members,) + block.shape)
    return lax.all_to_all(copies, axes, 0, 0, tiled=True)


def two_terms(values):
    high = values.astype(jnp.bfloat16)
    return high, (values - high.astype(jnp.float32)).astype(jnp.bfloat16)


def gather_codes(codebook):
    width = codebook.shape[1]
    across = lax.axis_size("x")
    pieces = lax.axis_size("h")
    blocks = [codebook]
    for step in range(1, across):
        ring = [(i, (i + step) % across) for i in range(across)]
        blocks.append(lax.ppermute(codebook, "x", ring))
    doubled = jnp.stack(blocks[::-1] * 2)
    first = across - 1 - lax.axis_index("x")
    own = lax.dynamic_slice_in_dim(doubled, first, across)
    other = lax.ppermute(own, "c", [(0, 1), (1, 0)])
    zero = lax.axis_index("c") == 0
    both = jnp.stack([jnp.where(zero, own, other), jnp.where(zero, other, own)], axis=1)
    both = both.reshape(across * 2, pieces, -1, width)
    return both.transpose(1, 0, 2, 3)


def shards(residuals, codebook):
    rows, width = residuals.shape
    pieces = lax.axis_size("h")
    depth = lax.axis_size("z")
    groups = lax.axis_size(ITEM_AXES)
    items = rows * pieces * depth
    share = codebook.shape[0] // lax.axis_size(("h", "l"))
    codes = codebook.shape[0] * lax.axis_size(("x", "c"))
    piece = lax.axis_index("h").astype(jnp.uint32)
    first = piece * (rows * depth)
    own_at = first + lax.axis_index("z").astype(jnp.uint32) * rows
    gathered = spread(residuals, ("h", "z")).reshape(items, width)
    codebook = gather_codes(codebook).reshape(pieces, -1, width)
    codes_float = codebook.astype(jnp.float32)
    code_scale = lax.rsqrt(jnp.mean(codes_float * codes_float, axis=2) + EPSILON)
    code_scale, piece, first, own_at = lax.optimization_barrier(
        (code_scale, piece, first, own_at)
    )
    rows_float = gathered.astype(jnp.float32)
    row_scale = lax.rsqrt(jnp.mean(rows_float * rows_float, axis=1) + EPSILON)
    row_scale = row_scale * (SHARPNESS / width)

    def kernel_of(codes, scales):
        similarity = jnp.einsum("nd,...kd->...nk", gathered, codes, preferred_element_type=jnp.float32)
        return jnp.exp(similarity * row_scale[:, None] * scales[..., None, :])

    kernel = kernel_of(codebook, code_scale).astype(jnp.bfloat16)
    own_kernel = kernel_of(
        lax.dynamic_index_in_dim(codebook, piece, keepdims=False),
        lax.dynamic_index_in_dim(code_scale, piece, keepdims=False),
    )
    kernel, own_kernel = lax.optimization_barrier((kernel, own_kernel))
    balance = (items * groups) / (codes * depth)
    weights_rows = None
    for sweep in range(ITERS):
        scaled = kernel.astype(jnp.float32)
        if weights_rows is not None:
            scaled = scaled * weights_rows[None, :, None]
        column_total = jnp.sum(spread(jnp.sum(scaled, axis=1), ITEM_AXES), axis=0)
        weights_cols = balance / column_total
        row_part = jnp.sum(
            kernel.astype(jnp.float32) * weights_cols[:, None, :], axis=(0, 2)
        )
        if sweep < ITERS - 1:
            row_total = jnp.sum(spread(row_part, "z"), axis=0)
            weights_rows = 1.0 / row_total

    mine = lax.dynamic_slice_in_dim(kernel, first, rows * depth, axis=1)
    shares = (mine.astype(jnp.float32) * weights_cols[:, None, :]).astype(jnp.bfloat16)
    products = jnp.einsum(
        "pnk,pkd->nd", shares, codebook, preferred_element_type=jnp.float32
    )
    products = products.astype(jnp.bfloat16).reshape(depth, rows, width)
    terms = jnp.concatenate([t.reshape(-1, width) for t in two_terms(row_part)])
    extra = terms.shape[0]
    terms = jnp.pad(terms, ((0, -extra % 8), (0, 0)))
    terms = jnp.broadcast_to(terms[None], (depth,) + terms.shape)
    packed = jnp.concatenate([products, terms], axis=1)
    weights_cols = lax.dynamic_index_in_dim(weights_cols, piece, keepdims=False)
    packed, weights_cols = lax.optimization_barrier((packed, weights_cols))
    packed = lax.all_to_all(packed, "z", 0, 0, tiled=True)
    total = jnp.sum(packed.astype(jnp.float32), axis=0)
    middle = rows + extra // 2
    row_total = total[rows:middle] + total[middle : rows + extra]
    weights_rows = 1.0 / row_total.reshape(items)

    transport = (own_kernel * weights_rows[:, None] * weights_cols[None, :]).astype(jnp.bfloat16)
    numerator = lax.dot_general(
        transport, gathered, (((0,), (0,)), ((), ())), preferred_element_type=jnp.float32
    )
    mass = jnp.sum(transport.astype(jnp.float32), axis=0)
    masses = jnp.stack([t.reshape(groups, share) for t in two_terms(mass)], axis=1)
    masses = jnp.pad(masses, ((0, 0), (0, 6), (0, width - share)))
    packed = jnp.concatenate(
        [numerator.astype(jnp.bfloat16).reshape(groups, share, width), masses], axis=1
    )
    packed = lax.all_to_all(packed, ITEM_AXES, 0, 0, tiled=True)

    own = lax.dynamic_slice_in_dim(weights_rows, own_at, rows)
    following = residuals.astype(jnp.float32) - total[:rows] * own[:, None]

    total = jnp.sum(packed.astype(jnp.float32), axis=0)
    mass_total = total[share, :share] + total[share + 1, :share]
    means = total[:share] / mass_total[:, None]
    new_codebook = spread(means.astype(MEANS), ("h", "l")).reshape(-1, width)
    new_codebook = new_codebook.astype(jnp.float32)
    return (new_codebook, following)


def solution(mesh):
    fine = Mesh(mesh.devices.reshape(4, 2, 4, 8, 2), ("h", "l", "x", "z", "c"))
    return jax.shard_map(
        shards,
        mesh=fine,
        in_specs=(P(("h", "l", "x", "z", "c"), None), P(("x", "z", "c"), None)),
        out_specs=(P(("x", "z", "c"), None), P(("h", "l", "x", "z", "c"), None)),
        check_vma=False,
    )
```

```python
import jax
import jax.numpy as jnp
from jax import lax
from jax.sharding import Mesh, PartitionSpec as P

ITERS = 3
EPSILON = 1e-06
SHARPNESS = 40.0
MEANS = jnp.float16

ITEM_AXES = ("x", "c", "l")


def spread(block, axes):
    members = lax.axis_size(axes)
    copies = jnp.broadcast_to(block[None], (members,) + block.shape)
    return lax.all_to_all(copies, axes, 0, 0, tiled=True)


def two_terms(values):
    high = values.astype(jnp.bfloat16)
    return high, (values - high.astype(jnp.float32)).astype(jnp.bfloat16)


def turned(array, start, axis):
    count = array.shape[axis]
    return jnp.stack(
        [
            lax.dynamic_index_in_dim(array, (start + step) % count, axis, keepdims=False)
            for step in range(count)
        ]
    )


def ordered(first, mine, other):
    return jnp.concatenate([jnp.where(first, mine, other), jnp.where(first, other, mine)])


def gather_codes(codebook, piece):
    width = codebook.shape[1]
    pieces = lax.axis_size("h")
    place = lax.axis_index("x")
    block = codebook[None]
    other = lax.ppermute(block, "x", [(0, 1), (1, 0), (2, 3), (3, 2)])
    block = ordered(place % 2 == 0, block, other)
    other = lax.ppermute(block, "x", [(0, 3), (3, 0), (1, 2), (2, 1)])
    block = ordered(place < 2, block, other)
    other = lax.ppermute(block, "c", [(0, 1), (1, 0)])
    zero = lax.axis_index("c") == 0
    both = jnp.stack([jnp.where(zero, block, other), jnp.where(zero, other, block)], axis=1)
    both = both.reshape(block.shape[0] * 2, pieces, -1, width)
    return turned(both, piece, 1).reshape(pieces, -1, width)


def shards(residuals, codebook):
    rows, width = residuals.shape
    pieces = lax.axis_size("h")
    depth = lax.axis_size("z")
    groups = lax.axis_size(ITEM_AXES)
    items = rows * pieces * depth
    share = codebook.shape[0] // lax.axis_size(("h", "l"))
    codes = codebook.shape[0] * lax.axis_size(("x", "c"))
    piece = lax.axis_index("h").astype(jnp.uint32)
    own_at = lax.axis_index("z").astype(jnp.uint32) * rows
    gathered = spread(residuals, ("h", "z")).reshape(pieces, -1, width)
    codebook = gather_codes(codebook, piece)
    codes_float = codebook.astype(jnp.float32)
    code_scale = lax.rsqrt(jnp.mean(codes_float * codes_float, axis=2) + EPSILON)
    code_scale, own_at = lax.optimization_barrier((code_scale, own_at))
    gathered = turned(gathered, piece, 0).reshape(items, width)
    rows_float = gathered.astype(jnp.float32)
    row_scale = lax.rsqrt(jnp.mean(rows_float * rows_float, axis=1) + EPSILON)
    row_scale = row_scale * (SHARPNESS / width)

    def kernel_of(codes, scales):
        similarity = jnp.einsum("nd,...kd->...nk", gathered, codes, preferred_element_type=jnp.float32)
        return jnp.exp(similarity * row_scale[:, None] * scales[..., None, :])

    own_kernel = kernel_of(codebook[0], code_scale[0])
    kernel = kernel_of(codebook[1:], code_scale[1:]).astype(jnp.bfloat16)
    own_kernel, kernel = lax.optimization_barrier((own_kernel, kernel))
    balance = (items * groups) / (codes * depth)
    weights_rows = None
    for sweep in range(ITERS):
        own, rest = own_kernel, kernel.astype(jnp.float32)
        if weights_rows is not None:
            own, rest = own * weights_rows[:, None], rest * weights_rows[None, :, None]
        column_part = jnp.concatenate([jnp.sum(own, axis=0)[None], jnp.sum(rest, axis=1)])
        column_total = jnp.sum(spread(column_part, ITEM_AXES), axis=0)
        weights_cols = balance / column_total
        row_part = jnp.sum(own_kernel * weights_cols[0][None, :], axis=1) + jnp.sum(
            kernel.astype(jnp.float32) * weights_cols[1:][:, None, :], axis=(0, 2)
        )
        if sweep < ITERS - 1:
            row_total = jnp.sum(spread(row_part, "z"), axis=0)
            weights_rows = 1.0 / row_total

    size = rows * depth
    own_kernel, kernel, weights_cols = lax.optimization_barrier((own_kernel, kernel, weights_cols))
    mine = own_kernel[:size] * weights_cols[0][None, :]
    rest = kernel[:, :size].astype(jnp.float32) * weights_cols[1:][:, None, :]
    products = jnp.dot(
        mine.astype(jnp.bfloat16), codebook[0], preferred_element_type=jnp.float32
    ) + jnp.einsum(
        "pnk,pkd->nd",
        rest.astype(jnp.bfloat16),
        codebook[1:],
        preferred_element_type=jnp.float32,
    )
    products = products.astype(jnp.bfloat16).reshape(depth, rows, width)
    terms = jnp.concatenate([t.reshape(-1, width) for t in two_terms(row_part)])
    extra = terms.shape[0]
    terms = jnp.pad(terms, ((0, -extra % 8), (0, 0)))
    terms = jnp.broadcast_to(terms[None], (depth,) + terms.shape)
    packed = jnp.concatenate([products, terms], axis=1)
    packed, weights_cols = lax.optimization_barrier((packed, weights_cols[0]))
    packed = lax.all_to_all(packed, "z", 0, 0, tiled=True)
    total = jnp.sum(packed.astype(jnp.float32), axis=0)
    middle = rows + extra // 2
    row_total = total[rows:middle] + total[middle : rows + extra]
    weights_rows = 1.0 / row_total.reshape(items)

    transport = (own_kernel * weights_rows[:, None] * weights_cols[None, :]).astype(jnp.bfloat16)
    numerator = lax.dot_general(
        transport, gathered, (((0,), (0,)), ((), ())), preferred_element_type=jnp.float32
    )
    mass = jnp.sum(transport.astype(jnp.float32), axis=0)
    masses = jnp.stack([t.reshape(groups, share) for t in two_terms(mass)], axis=1)
    masses = jnp.pad(masses, ((0, 0), (0, 6), (0, width - share)))
    packed = jnp.concatenate(
        [numerator.astype(jnp.bfloat16).reshape(groups, share, width), masses], axis=1
    )
    packed = lax.all_to_all(packed, ITEM_AXES, 0, 0, tiled=True)

    own = lax.dynamic_slice_in_dim(weights_rows, own_at, rows)
    following = residuals.astype(jnp.float32) - total[:rows] * own[:, None]

    total = jnp.sum(packed.astype(jnp.float32), axis=0)
    mass_total = total[share, :share] + total[share + 1, :share]
    means = total[:share] / mass_total[:, None]
    new_codebook = spread(means.astype(MEANS), ("h", "l")).reshape(-1, width)
    new_codebook = new_codebook.astype(jnp.float32)
    return (new_codebook, following)


def solution(mesh):
    fine = Mesh(mesh.devices.reshape(4, 2, 4, 8, 2), ("h", "l", "x", "z", "c"))
    return jax.shard_map(
        shards,
        mesh=fine,
        in_specs=(P(("h", "l", "x", "z", "c"), None), P(("x", "z", "c"), None)),
        out_specs=(P(("x", "z", "c"), None), P(("h", "l", "x", "z", "c"), None)),
        check_vma=False,
    )
```

```python
import jax
import jax.numpy as jnp
from jax import lax
from jax.sharding import Mesh, PartitionSpec as P

ITERS = 3
EPSILON = 1e-06
SHARPNESS = 40.0
MEANS = jnp.float16

ITEM_AXES = ("x", "c", "l")


def spread(block, axes):
    members = lax.axis_size(axes)
    copies = jnp.broadcast_to(block[None], (members,) + block.shape)
    return lax.all_to_all(copies, axes, 0, 0, tiled=True)


def two_terms(values):
    high = values.astype(jnp.bfloat16)
    return high, (values - high.astype(jnp.float32)).astype(jnp.bfloat16)


def turned(array, start, axis):
    count = array.shape[axis]
    return jnp.stack(
        [
            lax.dynamic_index_in_dim(array, (start + step) % count, axis, keepdims=False)
            for step in range(count)
        ]
    )


def gather_codes(codebook, piece):
    width = codebook.shape[1]
    pieces = lax.axis_size("h")
    across = lax.axis_size("x")
    place, core = lax.axis_index("x"), lax.axis_index("c")
    pairs = ([1, 0, 3, 2], [3, 2, 1, 0])

    def swap(block, turn):
        return lax.ppermute(
            block,
            ("x", "c"),
            [(x * 2 + c, pairs[turn ^ c][x] * 2 + c) for x in range(across) for c in range(2)],
        )

    other = swap(codebook, 0)
    block = jnp.stack([codebook, other])
    other = swap(block, 1)
    block = jnp.concatenate([block, other])
    near, far = place ^ 1, across - 1 - place
    held = [
        jnp.where(
            x == place,
            0,
            jnp.where(x == near, 1 + core, jnp.where(x == far, 2 - core, 3)),
        )
        for x in range(across)
    ]
    block = jnp.stack([lax.dynamic_index_in_dim(block, at, keepdims=False) for at in held])
    other = lax.ppermute(block, "c", [(0, 1), (1, 0)])
    zero = core == 0
    both = jnp.stack([jnp.where(zero, block, other), jnp.where(zero, other, block)], axis=1)
    both = both.reshape(across * 2, pieces, -1, width)
    return turned(both, piece, 1).reshape(pieces, -1, width)


def shards(residuals, codebook):
    rows, width = residuals.shape
    pieces = lax.axis_size("h")
    depth = lax.axis_size("z")
    groups = lax.axis_size(ITEM_AXES)
    items = rows * pieces * depth
    share = codebook.shape[0] // lax.axis_size(("h", "l"))
    codes = codebook.shape[0] * lax.axis_size(("x", "c"))
    piece = lax.axis_index("h").astype(jnp.uint32)
    own_at = lax.axis_index("z").astype(jnp.uint32) * rows
    gathered = spread(residuals, ("h", "z")).reshape(pieces, -1, width)
    codebook = gather_codes(codebook, piece)
    codes_float = codebook.astype(jnp.float32)
    code_scale = lax.rsqrt(jnp.mean(codes_float * codes_float, axis=2) + EPSILON)
    code_scale, own_at = lax.optimization_barrier((code_scale, own_at))
    gathered = turned(gathered, piece, 0).reshape(items, width)
    rows_float = gathered.astype(jnp.float32)
    row_scale = lax.rsqrt(jnp.mean(rows_float * rows_float, axis=1) + EPSILON)
    row_scale = row_scale * (SHARPNESS / width)

    def kernel_of(codes, scales):
        similarity = jnp.einsum("nd,...kd->...nk", gathered, codes, preferred_element_type=jnp.float32)
        return jnp.exp(similarity * row_scale[:, None] * scales[..., None, :])

    own_kernel = kernel_of(codebook[0], code_scale[0])
    kernel = kernel_of(codebook[1:], code_scale[1:]).astype(jnp.bfloat16)
    own_kernel, kernel = lax.optimization_barrier((own_kernel, kernel))
    balance = (items * groups) / (codes * depth)
    weights_rows = None
    for sweep in range(ITERS):
        own, rest = own_kernel, kernel.astype(jnp.float32)
        if weights_rows is not None:
            own, rest = own * weights_rows[:, None], rest * weights_rows[None, :, None]
        column_part = jnp.concatenate([jnp.sum(own, axis=0)[None], jnp.sum(rest, axis=1)])
        column_part = lax.optimization_barrier(column_part)
        column_parts = spread(column_part.astype(jnp.bfloat16), ITEM_AXES)
        column_total = jnp.sum(column_parts.astype(jnp.float32), axis=0)
        weights_cols = balance / column_total
        row_part = jnp.sum(own_kernel * weights_cols[0][None, :], axis=1) + jnp.sum(
            kernel.astype(jnp.float32) * weights_cols[1:][:, None, :], axis=(0, 2)
        )
        if sweep < ITERS - 1:
            row_total = jnp.sum(spread(row_part, "z"), axis=0)
            weights_rows = 1.0 / row_total

    size = rows * depth
    own_kernel, kernel, weights_cols = lax.optimization_barrier((own_kernel, kernel, weights_cols))
    products = 0.0
    for part in range(pieces):
        mine = own_kernel[:size] if part == 0 else kernel[part - 1, :size]
        mine = mine.astype(jnp.float32) * weights_cols[part][None, :]
        products = products + jnp.dot(
            mine.astype(jnp.bfloat16), codebook[part], preferred_element_type=jnp.float32
        )
    products = products.astype(jnp.bfloat16).reshape(depth, rows, width)
    terms = jnp.concatenate([t.reshape(-1, width) for t in two_terms(row_part)])
    extra = terms.shape[0]
    terms = jnp.pad(terms, ((0, -extra % 8), (0, 0)))
    terms = jnp.broadcast_to(terms[None], (depth,) + terms.shape)
    packed = jnp.concatenate([products, terms], axis=1)
    packed, weights_cols = lax.optimization_barrier((packed, weights_cols[0]))
    packed = lax.all_to_all(packed, "z", 0, 0, tiled=True)
    total = jnp.sum(packed.astype(jnp.float32), axis=0)
    middle = rows + extra // 2
    row_total = total[rows:middle] + total[middle : rows + extra]
    weights_rows = 1.0 / row_total.reshape(items)

    transport = (own_kernel * weights_rows[:, None] * weights_cols[None, :]).astype(jnp.bfloat16)
    numerator = lax.dot_general(
        transport, gathered, (((0,), (0,)), ((), ())), preferred_element_type=jnp.float32
    )
    mass = jnp.sum(transport.astype(jnp.float32), axis=0)
    masses = jnp.stack([t.reshape(groups, share) for t in two_terms(mass)], axis=1)
    masses = jnp.pad(masses, ((0, 0), (0, 6), (0, width - share)))
    packed = jnp.concatenate(
        [numerator.astype(jnp.bfloat16).reshape(groups, share, width), masses], axis=1
    )
    packed = lax.all_to_all(packed, ITEM_AXES, 0, 0, tiled=True)

    own = lax.dynamic_slice_in_dim(weights_rows, own_at, rows)
    following = residuals.astype(jnp.float32) - total[:rows] * own[:, None]

    total = jnp.sum(packed.astype(jnp.float32), axis=0)
    mass_total = total[share, :share] + total[share + 1, :share]
    means = total[:share] / mass_total[:, None]
    new_codebook = spread(means.astype(MEANS), ("h", "l")).reshape(-1, width)
    new_codebook = new_codebook.astype(jnp.float32)
    return (new_codebook, following)


def solution(mesh):
    fine = Mesh(mesh.devices.reshape(4, 2, 4, 8, 2), ("h", "l", "x", "z", "c"))
    return jax.shard_map(
        shards,
        mesh=fine,
        in_specs=(P(("h", "l", "x", "z", "c"), None), P(("x", "z", "c"), None)),
        out_specs=(P(("x", "z", "c"), None), P(("h", "l", "x", "z", "c"), None)),
        check_vma=False,
    )
```

```python
import jax
import jax.numpy as jnp
from jax import lax
from jax.experimental import pallas as pl
from jax.experimental.pallas import tpu as pltpu
from jax.sharding import Mesh, PartitionSpec as P

ITERS = 3
EPSILON = 1e-06
SHARPNESS = 40.0
MEANS = jnp.float16

ITEM_AXES = ("x", "c", "l")


def spread(block, axes):
    members = lax.axis_size(axes)
    copies = jnp.broadcast_to(block[None], (members,) + block.shape)
    return lax.all_to_all(copies, axes, 0, 0, tiled=True)


def prepare_kernel(rows_ref, codes_ref, copies_ref, held_ref, block, sems, codes_sem):
    keep = pltpu.make_async_copy(codes_ref, held_ref, codes_sem)
    keep.start()
    members = copies_ref.shape[0]
    read = pltpu.make_async_copy(rows_ref, block, sems.at[members])
    read.start()
    read.wait()
    writes = [
        pltpu.make_async_copy(block, copies_ref.at[member], sems.at[member])
        for member in range(members)
    ]
    for write in writes:
        write.start()
    for write in writes:
        write.wait()
    keep.wait()


def prepare(residuals, codebook, members):
    return pl.pallas_call(
        prepare_kernel,
        out_shape=(
            jax.ShapeDtypeStruct((members,) + residuals.shape, residuals.dtype),
            jax.ShapeDtypeStruct(codebook.shape, codebook.dtype),
        ),
        in_specs=[pl.BlockSpec(memory_space=pl.ANY)] * 2,
        out_specs=(pl.BlockSpec(memory_space=pl.ANY), pl.BlockSpec(memory_space=pltpu.VMEM)),
        scratch_shapes=[
            pltpu.VMEM(residuals.shape, residuals.dtype),
            pltpu.SemaphoreType.DMA((members + 1,)),
            pltpu.SemaphoreType.DMA,
        ],
        compiler_params=pltpu.CompilerParams(vmem_limit_bytes=2**21),
    )(residuals, codebook)


def two_terms(values):
    high = values.astype(jnp.bfloat16)
    return high, (values - high.astype(jnp.float32)).astype(jnp.bfloat16)


def turned(array, start, axis):
    count = array.shape[axis]
    return jnp.stack(
        [
            lax.dynamic_index_in_dim(array, (start + step) % count, axis, keepdims=False)
            for step in range(count)
        ]
    )


def gather_codes(codebook, held, piece):
    width = codebook.shape[1]
    pieces = lax.axis_size("h")
    across = lax.axis_size("x")
    place, core = lax.axis_index("x"), lax.axis_index("c")
    pairs = ([1, 0, 3, 2], [3, 2, 1, 0])

    def swap(block, turn):
        return lax.ppermute(
            block,
            ("x", "c"),
            [(x * 2 + c, pairs[turn ^ c][x] * 2 + c) for x in range(across) for c in range(2)],
        )

    other = swap(codebook, 0)
    block = jnp.stack([held, other])
    other = swap(block, 1)
    block = jnp.concatenate([block, other])
    near, far = place ^ 1, across - 1 - place
    places = [
        jnp.where(
            x == place,
            0,
            jnp.where(x == near, 1 + core, jnp.where(x == far, 2 - core, 3)),
        )
        for x in range(across)
    ]
    block = jnp.stack([lax.dynamic_index_in_dim(block, at, keepdims=False) for at in places])
    other = lax.ppermute(block, "c", [(0, 1), (1, 0)])
    zero = core == 0
    both = jnp.stack([jnp.where(zero, block, other), jnp.where(zero, other, block)], axis=1)
    both = both.reshape(across * 2, pieces, -1, width)
    return turned(both, piece, 1).reshape(pieces, -1, width)


def shards(residuals, codebook):
    rows, width = residuals.shape
    pieces = lax.axis_size("h")
    depth = lax.axis_size("z")
    groups = lax.axis_size(ITEM_AXES)
    items = rows * pieces * depth
    share = codebook.shape[0] // lax.axis_size(("h", "l"))
    codes = codebook.shape[0] * lax.axis_size(("x", "c"))
    piece = lax.axis_index("h").astype(jnp.uint32)
    own_at = lax.axis_index("z").astype(jnp.uint32) * rows
    copies, held = prepare(residuals, codebook, pieces * depth)
    gathered = lax.all_to_all(copies, ("h", "z"), 0, 0, tiled=True)
    gathered = gathered.reshape(pieces, -1, width)
    codebook = gather_codes(codebook, held, piece)
    codes_float = codebook.astype(jnp.float32)
    code_scale = lax.rsqrt(jnp.mean(codes_float * codes_float, axis=2) + EPSILON)
    code_scale, own_scale, own_at = lax.optimization_barrier(
        (code_scale, code_scale[0], own_at)
    )
    gathered = turned(gathered, piece, 0).reshape(items, width)
    rows_float = gathered.astype(jnp.float32)
    row_scale = lax.rsqrt(jnp.mean(rows_float * rows_float, axis=1) + EPSILON)
    row_scale = row_scale * (SHARPNESS / width)

    def kernel_of(gathered, codes, scales):
        similarity = jnp.einsum(
            "nd,...kd->...nk", gathered, codes, preferred_element_type=jnp.float32
        )
        return jnp.exp(similarity * row_scale[:, None] * scales[..., None, :])

    kernel = kernel_of(gathered, codebook, code_scale).astype(jnp.bfloat16)
    kernel = lax.optimization_barrier(kernel)
    balance = (items * groups) / (codes * depth)
    weights_rows = None
    for sweep in range(ITERS):
        scaled = kernel.astype(jnp.float32)
        if weights_rows is not None:
            scaled = scaled * weights_rows[None, :, None]
        column_part = lax.optimization_barrier(jnp.sum(scaled, axis=1))
        column_parts = spread(column_part.astype(jnp.bfloat16), ITEM_AXES)
        column_total = jnp.sum(column_parts.astype(jnp.float32), axis=0)
        weights_cols = balance / column_total
        row_part = jnp.sum(
            kernel.astype(jnp.float32) * weights_cols[:, None, :], axis=(0, 2)
        )
        if sweep < ITERS - 1:
            row_total = jnp.sum(spread(row_part, "z"), axis=0)
            weights_rows = 1.0 / row_total

    size = rows * depth
    mine = kernel[:, :size].astype(jnp.float32) * weights_cols[:, None, :]
    products = jnp.einsum(
        "pnk,pkd->nd", mine.astype(jnp.bfloat16), codebook, preferred_element_type=jnp.float32
    )
    products = products.astype(jnp.bfloat16).reshape(depth, rows, width)
    terms = jnp.concatenate([t.reshape(-1, width) for t in two_terms(row_part)])
    extra = terms.shape[0]
    terms = jnp.pad(terms, ((0, -extra % 8), (0, 0)))
    terms = jnp.broadcast_to(terms[None], (depth,) + terms.shape)
    packed = jnp.concatenate([products, terms], axis=1)
    packed, weights_cols = lax.optimization_barrier((packed, weights_cols[0]))
    packed = lax.all_to_all(packed, "z", 0, 0, tiled=True)
    total = jnp.sum(packed.astype(jnp.float32), axis=0)
    middle = rows + extra // 2
    row_total = total[rows:middle] + total[middle : rows + extra]
    weights_rows = 1.0 / row_total.reshape(items)

    again, weights_rows = lax.optimization_barrier((gathered, weights_rows))
    own_kernel = kernel_of(again, codebook[0], own_scale)
    transport = (own_kernel * weights_rows[:, None] * weights_cols[None, :]).astype(jnp.bfloat16)
    numerator = lax.dot_general(
        transport, gathered, (((0,), (0,)), ((), ())), preferred_element_type=jnp.float32
    )
    mass = jnp.sum(transport.astype(jnp.float32), axis=0)
    masses = jnp.stack([t.reshape(groups, share) for t in two_terms(mass)], axis=1)
    masses = jnp.pad(masses, ((0, 0), (0, 6), (0, width - share)))
    packed = jnp.concatenate(
        [numerator.astype(jnp.bfloat16).reshape(groups, share, width), masses], axis=1
    )
    packed = lax.all_to_all(packed, ITEM_AXES, 0, 0, tiled=True)

    own = lax.dynamic_slice_in_dim(weights_rows, own_at, rows)
    following = residuals.astype(jnp.float32) - total[:rows] * own[:, None]

    total = jnp.sum(packed.astype(jnp.float32), axis=0)
    mass_total = total[share, :share] + total[share + 1, :share]
    means = total[:share] / mass_total[:, None]
    new_codebook = spread(means.astype(MEANS), ("h", "l")).reshape(-1, width)
    new_codebook = new_codebook.astype(jnp.float32)
    return (new_codebook, following)


def solution(mesh):
    fine = Mesh(mesh.devices.reshape(4, 2, 4, 8, 2), ("h", "l", "x", "z", "c"))
    return jax.shard_map(
        shards,
        mesh=fine,
        in_specs=(P(("h", "l", "x", "z", "c"), None), P(("x", "z", "c"), None)),
        out_specs=(P(("x", "z", "c"), None), P(("h", "l", "x", "z", "c"), None)),
        check_vma=False,
    )
```

```python
import jax
import jax.numpy as jnp
from jax import lax
from jax.experimental import pallas as pl
from jax.experimental.pallas import tpu as pltpu
from jax.sharding import Mesh, PartitionSpec as P

ITERS = 3
EPSILON = 1e-06
SHARPNESS = 40.0
MEANS = jnp.float16

ITEM_AXES = ("x", "c", "l")


def spread(block, axes):
    members = lax.axis_size(axes)
    copies = jnp.broadcast_to(block[None], (members,) + block.shape)
    return lax.all_to_all(copies, axes, 0, 0, tiled=True)


def copies_kernel(rows_ref, copies_ref, block, sems):
    members = copies_ref.shape[0]
    read = pltpu.make_async_copy(rows_ref, block, sems.at[members])
    read.start()
    read.wait()
    writes = [
        pltpu.make_async_copy(block, copies_ref.at[member], sems.at[member])
        for member in range(members)
    ]
    for write in writes:
        write.start()
    for write in writes:
        write.wait()


def copies_of(block, members):
    return pl.pallas_call(
        copies_kernel,
        out_shape=jax.ShapeDtypeStruct((members,) + block.shape, block.dtype),
        in_specs=[pl.BlockSpec(memory_space=pl.ANY)],
        out_specs=pl.BlockSpec(memory_space=pl.ANY),
        scratch_shapes=[
            pltpu.VMEM(block.shape, block.dtype),
            pltpu.SemaphoreType.DMA((members + 1,)),
        ],
    )(block)


def hold_kernel(block_ref, held_ref):
    held_ref[...] = block_ref[...]


def hold(block):
    return pl.pallas_call(
        hold_kernel,
        out_shape=jax.ShapeDtypeStruct(block.shape, block.dtype),
        compiler_params=pltpu.CompilerParams(vmem_limit_bytes=2**21),
    )(block)


def two_terms(values):
    high = values.astype(jnp.bfloat16)
    return high, (values - high.astype(jnp.float32)).astype(jnp.bfloat16)


def turned(array, start, axis):
    count = array.shape[axis]
    return jnp.stack(
        [
            lax.dynamic_index_in_dim(array, (start + step) % count, axis, keepdims=False)
            for step in range(count)
        ]
    )


def gather_codes(codebook, piece):
    width = codebook.shape[1]
    pieces = lax.axis_size("h")
    across = lax.axis_size("x")
    place, core = lax.axis_index("x"), lax.axis_index("c")
    pairs = ([1, 0, 3, 2], [3, 2, 1, 0])

    def swap(block, turn):
        return lax.ppermute(
            block,
            ("x", "c"),
            [(x * 2 + c, pairs[turn ^ c][x] * 2 + c) for x in range(across) for c in range(2)],
        )

    first = swap(codebook, 0)
    second = swap(codebook, 1)
    third = swap(first, 1)
    own = hold(codebook)
    block = jnp.stack([own, first, second, third])
    near, far = place ^ 1, across - 1 - place
    places = [
        jnp.where(
            x == place,
            0,
            jnp.where(x == near, 1 + core, jnp.where(x == far, 2 - core, 3)),
        )
        for x in range(across)
    ]
    block = jnp.stack([lax.dynamic_index_in_dim(block, at, keepdims=False) for at in places])
    other = lax.ppermute(block, "c", [(0, 1), (1, 0)])
    zero = core == 0
    both = jnp.stack([jnp.where(zero, block, other), jnp.where(zero, other, block)], axis=1)
    both = both.reshape(across * 2, pieces, -1, width)
    return turned(both, piece, 1).reshape(pieces, -1, width)


def shards(residuals, codebook):
    rows, width = residuals.shape
    pieces = lax.axis_size("h")
    depth = lax.axis_size("z")
    groups = lax.axis_size(ITEM_AXES)
    items = rows * pieces * depth
    share = codebook.shape[0] // lax.axis_size(("h", "l"))
    codes = codebook.shape[0] * lax.axis_size(("x", "c"))
    piece = lax.axis_index("h").astype(jnp.uint32)
    own_at = lax.axis_index("z").astype(jnp.uint32) * rows
    copies = copies_of(residuals, pieces * depth)
    gathered = lax.all_to_all(copies, ("h", "z"), 0, 0, tiled=True)
    gathered = gathered.reshape(pieces, -1, width)
    codebook = gather_codes(codebook, piece)
    codes_float = codebook.astype(jnp.float32)
    code_scale = lax.rsqrt(jnp.mean(codes_float * codes_float, axis=2) + EPSILON)
    code_scale, own_scale, own_at = lax.optimization_barrier(
        (code_scale, code_scale[0], own_at)
    )
    gathered = turned(gathered, piece, 0).reshape(items, width)
    rows_float = gathered.astype(jnp.float32)
    row_scale = lax.rsqrt(jnp.mean(rows_float * rows_float, axis=1) + EPSILON)
    row_scale = row_scale * (SHARPNESS / width)

    def kernel_of(gathered, codes, scales):
        similarity = jnp.einsum(
            "nd,...kd->...nk", gathered, codes, preferred_element_type=jnp.float32
        )
        return jnp.exp(similarity * row_scale[:, None] * scales[..., None, :])

    kernel = kernel_of(gathered, codebook, code_scale).astype(jnp.bfloat16)
    kernel = lax.optimization_barrier(kernel)
    balance = (items * groups) / (codes * depth)
    weights_rows = None
    for sweep in range(ITERS):
        scaled = kernel.astype(jnp.float32)
        if weights_rows is not None:
            scaled = scaled * weights_rows[None, :, None]
        column_part = lax.optimization_barrier(jnp.sum(scaled, axis=1))
        column_parts = spread(column_part.astype(jnp.bfloat16), ITEM_AXES)
        column_total = jnp.sum(column_parts.astype(jnp.float32), axis=0)
        weights_cols = balance / column_total
        row_part = jnp.sum(
            kernel.astype(jnp.float32) * weights_cols[:, None, :], axis=(0, 2)
        )
        if sweep < ITERS - 1:
            row_total = jnp.sum(spread(row_part, "z"), axis=0)
            weights_rows = 1.0 / row_total

    size = rows * depth
    mine = kernel[:, :size].astype(jnp.float32) * weights_cols[:, None, :]
    products = jnp.einsum(
        "pnk,pkd->nd", mine.astype(jnp.bfloat16), codebook, preferred_element_type=jnp.float32
    )
    products = products.astype(jnp.bfloat16).reshape(depth, rows, width)
    terms = jnp.concatenate([t.reshape(-1, width) for t in two_terms(row_part)])
    extra = terms.shape[0]
    terms = jnp.pad(terms, ((0, -extra % 8), (0, 0)))
    terms = jnp.broadcast_to(terms[None], (depth,) + terms.shape)
    packed = jnp.concatenate([products, terms], axis=1)
    packed, weights_cols = lax.optimization_barrier((packed, weights_cols[0]))
    packed = lax.all_to_all(packed, "z", 0, 0, tiled=True)
    total = jnp.sum(packed.astype(jnp.float32), axis=0)
    middle = rows + extra // 2
    row_total = total[rows:middle] + total[middle : rows + extra]
    weights_rows = 1.0 / row_total.reshape(items)

    again, weights_rows = lax.optimization_barrier((gathered, weights_rows))
    own_kernel = kernel_of(again, codebook[0], own_scale)
    transport = (own_kernel * weights_rows[:, None] * weights_cols[None, :]).astype(jnp.bfloat16)
    numerator = lax.dot_general(
        transport, gathered, (((0,), (0,)), ((), ())), preferred_element_type=jnp.float32
    )
    mass = jnp.sum(transport.astype(jnp.float32), axis=0)
    masses = jnp.stack([t.reshape(groups, share) for t in two_terms(mass)], axis=1)
    masses = jnp.pad(masses, ((0, 0), (0, 6), (0, width - share)))
    packed = jnp.concatenate(
        [numerator.astype(jnp.bfloat16).reshape(groups, share, width), masses], axis=1
    )
    packed = lax.all_to_all(packed, ITEM_AXES, 0, 0, tiled=True)

    own = lax.dynamic_slice_in_dim(weights_rows, own_at, rows)
    following = residuals.astype(jnp.float32) - total[:rows] * own[:, None]

    total = jnp.sum(packed.astype(jnp.float32), axis=0)
    mass_total = total[share, :share] + total[share + 1, :share]
    means = total[:share] / mass_total[:, None]
    new_codebook = spread(means.astype(MEANS), ("h", "l")).reshape(-1, width)
    new_codebook = new_codebook.astype(jnp.float32)
    return (new_codebook, following)


def solution(mesh):
    fine = Mesh(mesh.devices.reshape(4, 2, 4, 8, 2), ("h", "l", "x", "z", "c"))
    return jax.shard_map(
        shards,
        mesh=fine,
        in_specs=(P(("h", "l", "x", "z", "c"), None), P(("x", "z", "c"), None)),
        out_specs=(P(("x", "z", "c"), None), P(("h", "l", "x", "z", "c"), None)),
        check_vma=False,
    )
```

```python
import jax
import jax.numpy as jnp
from jax import lax
from jax.experimental import pallas as pl
from jax.experimental.pallas import tpu as pltpu
from jax.sharding import Mesh, PartitionSpec as P

ITERS = 3
EPSILON = 1e-06
SHARPNESS = 40.0
MEANS = jnp.float16

ITEM_AXES = ("x", "c", "l")


def spread(block, axes):
    members = lax.axis_size(axes)
    copies = jnp.broadcast_to(block[None], (members,) + block.shape)
    return lax.all_to_all(copies, axes, 0, 0, tiled=True)


def hold_kernel(block_ref, held_ref):
    held_ref[...] = block_ref[...]


def hold(block):
    return pl.pallas_call(
        hold_kernel,
        out_shape=jax.ShapeDtypeStruct(block.shape, block.dtype),
        compiler_params=pltpu.CompilerParams(vmem_limit_bytes=2**21),
    )(block)


def two_terms(values):
    high = values.astype(jnp.bfloat16)
    return high, (values - high.astype(jnp.float32)).astype(jnp.bfloat16)


def turned(array, start, axis):
    count = array.shape[axis]
    return jnp.stack(
        [
            lax.dynamic_index_in_dim(array, (start + step) % count, axis, keepdims=False)
            for step in range(count)
        ]
    )


def gather_codes(codebook, held, piece):
    width = codebook.shape[1]
    pieces = lax.axis_size("h")
    across = lax.axis_size("x")
    place, core = lax.axis_index("x"), lax.axis_index("c")
    pairs = ([1, 0, 3, 2], [3, 2, 1, 0])

    def swap(block, turn):
        return lax.ppermute(
            block,
            ("x", "c"),
            [(x * 2 + c, pairs[turn ^ c][x] * 2 + c) for x in range(across) for c in range(2)],
        )

    other = swap(codebook, 0)
    block = jnp.stack([held, other])
    other = swap(block, 1)
    block = jnp.concatenate([block, other])
    near, far = place ^ 1, across - 1 - place
    places = [
        jnp.where(
            x == place,
            0,
            jnp.where(x == near, 1 + core, jnp.where(x == far, 2 - core, 3)),
        )
        for x in range(across)
    ]
    block = jnp.stack([lax.dynamic_index_in_dim(block, at, keepdims=False) for at in places])
    other = lax.ppermute(block, "c", [(0, 1), (1, 0)])
    zero = core == 0
    both = jnp.stack([jnp.where(zero, block, other), jnp.where(zero, other, block)], axis=1)
    both = both.reshape(across * 2, pieces, -1, width)
    return turned(both, piece, 1).reshape(pieces, -1, width)


def shards(residuals, codebook):
    rows, width = residuals.shape
    pieces = lax.axis_size("h")
    depth = lax.axis_size("z")
    groups = lax.axis_size(ITEM_AXES)
    items = rows * pieces * depth
    share = codebook.shape[0] // lax.axis_size(("h", "l"))
    codes = codebook.shape[0] * lax.axis_size(("x", "c"))
    piece = lax.axis_index("h").astype(jnp.uint32)
    own_at = lax.axis_index("z").astype(jnp.uint32) * rows
    gathered = spread(residuals, ("h", "z")).reshape(pieces, -1, width)
    held = hold(codebook)
    codebook = gather_codes(codebook, held, piece)
    codes_float = codebook.astype(jnp.float32)
    code_scale = lax.rsqrt(jnp.mean(codes_float * codes_float, axis=2) + EPSILON)
    code_scale, own_scale, own_at = lax.optimization_barrier(
        (code_scale, code_scale[0], own_at)
    )
    gathered = turned(gathered, piece, 0).reshape(items, width)
    rows_float = gathered.astype(jnp.float32)
    row_scale = lax.rsqrt(jnp.mean(rows_float * rows_float, axis=1) + EPSILON)
    row_scale = row_scale * (SHARPNESS / width)

    def kernel_of(gathered, codes, scales):
        similarity = jnp.einsum(
            "nd,...kd->...nk", gathered, codes, preferred_element_type=jnp.float32
        )
        return jnp.exp(similarity * row_scale[:, None] * scales[..., None, :])

    kernel = kernel_of(gathered, codebook, code_scale).astype(jnp.bfloat16)
    kernel = lax.optimization_barrier(kernel)
    balance = (items * groups) / (codes * depth)
    weights_rows = None
    for sweep in range(ITERS):
        scaled = kernel.astype(jnp.float32)
        if weights_rows is not None:
            scaled = scaled * weights_rows[None, :, None]
        column_part = lax.optimization_barrier(jnp.sum(scaled, axis=1))
        column_parts = spread(column_part.astype(jnp.bfloat16), ITEM_AXES)
        column_total = jnp.sum(column_parts.astype(jnp.float32), axis=0)
        weights_cols = balance / column_total
        row_part = jnp.sum(
            kernel.astype(jnp.float32) * weights_cols[:, None, :], axis=(0, 2)
        )
        if sweep < ITERS - 1:
            row_total = jnp.sum(spread(row_part, "z"), axis=0)
            weights_rows = 1.0 / row_total

    size = rows * depth
    mine = kernel[:, :size].astype(jnp.float32) * weights_cols[:, None, :]
    products = jnp.einsum(
        "pnk,pkd->nd", mine.astype(jnp.bfloat16), codebook, preferred_element_type=jnp.float32
    )
    products = products.astype(jnp.bfloat16).reshape(depth, rows, width)
    terms = jnp.concatenate([t.reshape(-1, width) for t in two_terms(row_part)])
    extra = terms.shape[0]
    terms = jnp.pad(terms, ((0, -extra % 8), (0, 0)))
    terms = jnp.broadcast_to(terms[None], (depth,) + terms.shape)
    packed = jnp.concatenate([products, terms], axis=1)
    packed, weights_cols = lax.optimization_barrier((packed, weights_cols[0]))
    packed = lax.all_to_all(packed, "z", 0, 0, tiled=True)
    total = jnp.sum(packed.astype(jnp.float32), axis=0)
    middle = rows + extra // 2
    row_total = total[rows:middle] + total[middle : rows + extra]
    weights_rows = 1.0 / row_total.reshape(items)

    again, weights_rows = lax.optimization_barrier((gathered, weights_rows))
    own_kernel = kernel_of(again, codebook[0], own_scale)
    transport = (own_kernel * weights_rows[:, None] * weights_cols[None, :]).astype(jnp.bfloat16)
    numerator = lax.dot_general(
        transport, gathered, (((0,), (0,)), ((), ())), preferred_element_type=jnp.float32
    )
    mass = jnp.sum(transport.astype(jnp.float32), axis=0)
    masses = jnp.stack([t.reshape(groups, share) for t in two_terms(mass)], axis=1)
    masses = jnp.pad(masses, ((0, 0), (0, 6), (0, width - share)))
    packed = jnp.concatenate(
        [numerator.astype(jnp.bfloat16).reshape(groups, share, width), masses], axis=1
    )
    packed = lax.all_to_all(packed, ITEM_AXES, 0, 0, tiled=True)

    own = lax.dynamic_slice_in_dim(weights_rows, own_at, rows)
    following = residuals.astype(jnp.float32) - total[:rows] * own[:, None]

    total = jnp.sum(packed.astype(jnp.float32), axis=0)
    mass_total = total[share, :share] + total[share + 1, :share]
    means = total[:share] / mass_total[:, None]
    new_codebook = spread(means.astype(MEANS), ("h", "l")).reshape(-1, width)
    new_codebook = new_codebook.astype(jnp.float32)
    return (new_codebook, following)


def solution(mesh):
    fine = Mesh(mesh.devices.reshape(4, 2, 4, 8, 2), ("h", "l", "x", "z", "c"))
    return jax.shard_map(
        shards,
        mesh=fine,
        in_specs=(P(("h", "l", "x", "z", "c"), None), P(("x", "z", "c"), None)),
        out_specs=(P(("x", "z", "c"), None), P(("h", "l", "x", "z", "c"), None)),
        check_vma=False,
    )
```

```python
import jax
import jax.numpy as jnp
from jax import lax
from jax.experimental import pallas as pl
from jax.experimental.pallas import tpu as pltpu
from jax.sharding import Mesh, PartitionSpec as P

ITERS = 3
EPSILON = 1e-06
SHARPNESS = 40.0
MEANS = jnp.float16

ITEM_AXES = ("x", "c", "l")


def spread(block, axes):
    members = lax.axis_size(axes)
    copies = jnp.broadcast_to(block[None], (members,) + block.shape)
    return lax.all_to_all(copies, axes, 0, 0, tiled=True)


def hold_kernel(block_ref, held_ref):
    held_ref[...] = block_ref[...]


def hold(block):
    return pl.pallas_call(
        hold_kernel,
        out_shape=jax.ShapeDtypeStruct(block.shape, block.dtype),
        compiler_params=pltpu.CompilerParams(vmem_limit_bytes=2**21),
    )(block)


def two_terms(values):
    high = values.astype(jnp.bfloat16)
    return high, (values - high.astype(jnp.float32)).astype(jnp.bfloat16)


def turned(array, start, axis):
    count = array.shape[axis]
    return jnp.stack(
        [
            lax.dynamic_index_in_dim(array, (start + step) % count, axis, keepdims=False)
            for step in range(count)
        ]
    )


def gather_codes(codebook, held, piece):
    width = codebook.shape[1]
    pieces = lax.axis_size("h")
    across = lax.axis_size("x")
    place, core = lax.axis_index("x"), lax.axis_index("c")
    pairs = ([1, 0, 3, 2], [3, 2, 1, 0])

    def swap(block, turn):
        return lax.ppermute(
            block,
            ("x", "c"),
            [(x * 2 + c, pairs[turn ^ c][x] * 2 + c) for x in range(across) for c in range(2)],
        )

    other = swap(codebook, 0)
    block = jnp.stack([held, other])
    last = swap(block, 1)
    other = lax.ppermute(block, "c", [(0, 1), (1, 0)])
    other_last = lax.ppermute(last, "c", [(0, 1), (1, 0)])

    def in_order(block, core):
        near, far = place ^ 1, across - 1 - place
        places = [
            jnp.where(
                x == place,
                0,
                jnp.where(x == near, 1 + core, jnp.where(x == far, 2 - core, 3)),
            )
            for x in range(across)
        ]
        return jnp.stack(
            [lax.dynamic_index_in_dim(block, at, keepdims=False) for at in places]
        )

    block = in_order(jnp.concatenate([block, last]), core)
    other = in_order(jnp.concatenate([other, other_last]), 1 - core)
    zero = core == 0
    both = jnp.stack([jnp.where(zero, block, other), jnp.where(zero, other, block)], axis=1)
    both = both.reshape(across * 2, pieces, -1, width)
    return turned(both, piece, 1).reshape(pieces, -1, width)


def shards(residuals, codebook):
    rows, width = residuals.shape
    pieces = lax.axis_size("h")
    depth = lax.axis_size("z")
    groups = lax.axis_size(ITEM_AXES)
    items = rows * pieces * depth
    share = codebook.shape[0] // lax.axis_size(("h", "l"))
    codes = codebook.shape[0] * lax.axis_size(("x", "c"))
    piece = lax.axis_index("h").astype(jnp.uint32)
    own_at = lax.axis_index("z").astype(jnp.uint32) * rows
    gathered = spread(residuals, ("h", "z")).reshape(pieces, -1, width)
    held = hold(codebook)
    codebook = gather_codes(codebook, held, piece)
    codes_float = codebook.astype(jnp.float32)
    code_scale = lax.rsqrt(jnp.mean(codes_float * codes_float, axis=2) + EPSILON)
    code_scale, own_scale, own_at = lax.optimization_barrier(
        (code_scale, code_scale[0], own_at)
    )
    gathered = turned(gathered, piece, 0).reshape(items, width)
    rows_float = gathered.astype(jnp.float32)
    row_scale = lax.rsqrt(jnp.mean(rows_float * rows_float, axis=1) + EPSILON)
    row_scale = row_scale * (SHARPNESS / width)

    def kernel_of(gathered, codes, scales):
        similarity = jnp.einsum(
            "nd,...kd->...nk", gathered, codes, preferred_element_type=jnp.float32
        )
        return jnp.exp(similarity * row_scale[:, None] * scales[..., None, :])

    kernel = kernel_of(gathered, codebook, code_scale).astype(jnp.bfloat16)
    kernel = lax.optimization_barrier(kernel)
    balance = (items * groups) / (codes * depth)
    weights_rows = None
    for sweep in range(ITERS):
        scaled = kernel.astype(jnp.float32)
        if weights_rows is not None:
            scaled = scaled * weights_rows[None, :, None]
        column_part = lax.optimization_barrier(jnp.sum(scaled, axis=1))
        column_parts = spread(column_part.astype(jnp.bfloat16), ITEM_AXES)
        column_total = jnp.sum(column_parts.astype(jnp.float32), axis=0)
        weights_cols = balance / column_total
        row_part = jnp.sum(
            kernel.astype(jnp.float32) * weights_cols[:, None, :], axis=(0, 2)
        )
        if sweep < ITERS - 1:
            row_total = jnp.sum(spread(row_part, "z"), axis=0)
            weights_rows = 1.0 / row_total

    size = rows * depth
    mine = kernel[:, :size].astype(jnp.float32) * weights_cols[:, None, :]
    products = jnp.einsum(
        "pnk,pkd->nd", mine.astype(jnp.bfloat16), codebook, preferred_element_type=jnp.float32
    )
    products = products.astype(jnp.bfloat16).reshape(depth, rows, width)
    terms = jnp.concatenate([t.reshape(-1, width) for t in two_terms(row_part)])
    extra = terms.shape[0]
    terms = jnp.pad(terms, ((0, -extra % 8), (0, 0)))
    terms = jnp.broadcast_to(terms[None], (depth,) + terms.shape)
    packed = jnp.concatenate([products, terms], axis=1)
    packed, weights_cols = lax.optimization_barrier((packed, weights_cols[0]))
    packed = lax.all_to_all(packed, "z", 0, 0, tiled=True)
    total = jnp.sum(packed.astype(jnp.float32), axis=0)
    middle = rows + extra // 2
    row_total = total[rows:middle] + total[middle : rows + extra]
    weights_rows = 1.0 / row_total.reshape(items)

    again, weights_rows = lax.optimization_barrier((gathered, weights_rows))
    own_kernel = kernel_of(again, codebook[0], own_scale)
    transport = (own_kernel * weights_rows[:, None] * weights_cols[None, :]).astype(jnp.bfloat16)
    numerator = lax.dot_general(
        transport, gathered, (((0,), (0,)), ((), ())), preferred_element_type=jnp.float32
    )
    mass = jnp.sum(transport.astype(jnp.float32), axis=0)
    masses = jnp.stack([t.reshape(groups, share) for t in two_terms(mass)], axis=1)
    masses = jnp.pad(masses, ((0, 0), (0, 6), (0, width - share)))
    packed = jnp.concatenate(
        [numerator.astype(jnp.bfloat16).reshape(groups, share, width), masses], axis=1
    )
    packed = lax.all_to_all(packed, ITEM_AXES, 0, 0, tiled=True)

    own = lax.dynamic_slice_in_dim(weights_rows, own_at, rows)
    following = residuals.astype(jnp.float32) - total[:rows] * own[:, None]

    total = jnp.sum(packed.astype(jnp.float32), axis=0)
    mass_total = total[share, :share] + total[share + 1, :share]
    means = total[:share] / mass_total[:, None]
    new_codebook = spread(means.astype(MEANS), ("h", "l")).reshape(-1, width)
    new_codebook = new_codebook.astype(jnp.float32)
    return (new_codebook, following)


def solution(mesh):
    fine = Mesh(mesh.devices.reshape(4, 2, 4, 8, 2), ("h", "l", "x", "z", "c"))
    return jax.shard_map(
        shards,
        mesh=fine,
        in_specs=(P(("h", "l", "x", "z", "c"), None), P(("x", "z", "c"), None)),
        out_specs=(P(("x", "z", "c"), None), P(("h", "l", "x", "z", "c"), None)),
        check_vma=False,
    )
```

```python
import jax
import jax.numpy as jnp
from jax import lax
from jax.experimental import pallas as pl
from jax.experimental.pallas import tpu as pltpu
from jax.sharding import Mesh, PartitionSpec as P

ITERS = 3
EPSILON = 1e-06
SHARPNESS = 40.0
MEANS = jnp.float16

ITEM_AXES = ("x", "c", "l")


def spread(block, axes):
    members = lax.axis_size(axes)
    copies = jnp.broadcast_to(block[None], (members,) + block.shape)
    return lax.all_to_all(copies, axes, 0, 0, tiled=True)


def hold_kernel(block_ref, held_ref):
    held_ref[...] = block_ref[...]


def hold(block):
    return pl.pallas_call(
        hold_kernel,
        out_shape=jax.ShapeDtypeStruct(block.shape, block.dtype),
        compiler_params=pltpu.CompilerParams(vmem_limit_bytes=2**21),
    )(block)


def two_terms(values):
    high = values.astype(jnp.bfloat16)
    return high, (values - high.astype(jnp.float32)).astype(jnp.bfloat16)


def turned(array, start, axis):
    count = array.shape[axis]
    return jnp.stack(
        [
            lax.dynamic_index_in_dim(array, (start + step) % count, axis, keepdims=False)
            for step in range(count)
        ]
    )


def gather_codes(codebook, held, piece):
    width = codebook.shape[1]
    pieces = lax.axis_size("h")
    across = lax.axis_size("x")
    place, core = lax.axis_index("x"), lax.axis_index("c")
    pairs = ([1, 0, 3, 2], [3, 2, 1, 0])

    def swap(block, turn):
        return lax.ppermute(
            block,
            ("x", "c"),
            [(x * 2 + c, pairs[turn ^ c][x] * 2 + c) for x in range(across) for c in range(2)],
        )

    other = swap(codebook, 0)
    block = jnp.stack([held, other])
    last = swap(block, 1)
    other = lax.ppermute(block, "c", [(0, 1), (1, 0)])
    other_last = lax.ppermute(last, "c", [(0, 1), (1, 0)])

    def in_order(block, core):
        near, far = place ^ 1, across - 1 - place
        places = [
            jnp.where(
                x == place,
                0,
                jnp.where(x == near, 1 + core, jnp.where(x == far, 2 - core, 3)),
            )
            for x in range(across)
        ]
        return jnp.stack(
            [lax.dynamic_index_in_dim(block, at, keepdims=False) for at in places]
        )

    block = in_order(jnp.concatenate([block, last]), core)
    other = in_order(jnp.concatenate([other, other_last]), 1 - core)
    zero = core == 0
    both = jnp.stack([jnp.where(zero, block, other), jnp.where(zero, other, block)], axis=1)
    both = both.reshape(across * 2, pieces, -1, width)
    return turned(both, piece, 1).reshape(pieces, -1, width)


def shards(residuals, codebook):
    rows, width = residuals.shape
    pieces = lax.axis_size("h")
    depth = lax.axis_size("z")
    groups = lax.axis_size(ITEM_AXES)
    items = rows * pieces * depth
    share = codebook.shape[0] // lax.axis_size(("h", "l"))
    codes = codebook.shape[0] * lax.axis_size(("x", "c"))
    piece = lax.axis_index("h").astype(jnp.uint32)
    own_at = lax.axis_index("z").astype(jnp.uint32) * rows
    gathered = spread(residuals, ("h", "z")).reshape(pieces, -1, width)
    held = hold(codebook)
    codebook = gather_codes(codebook, held, piece)
    codes_float = codebook.astype(jnp.float32)
    code_scale = lax.rsqrt(jnp.mean(codes_float * codes_float, axis=2) + EPSILON)
    code_scale, own_scale, own_at = lax.optimization_barrier(
        (code_scale, code_scale[0], own_at)
    )
    gathered = turned(gathered, piece, 0).reshape(items, width)
    rows_float = gathered.astype(jnp.float32)
    row_scale = lax.rsqrt(jnp.mean(rows_float * rows_float, axis=1) + EPSILON)
    row_scale = row_scale * (SHARPNESS / width)

    def kernel_of(gathered, codes, scales):
        similarity = jnp.einsum(
            "nd,...kd->...nk", gathered, codes, preferred_element_type=jnp.float32
        )
        return jnp.exp(similarity * row_scale[:, None] * scales[..., None, :])

    kernel = kernel_of(gathered, codebook, code_scale).astype(jnp.bfloat16)
    kernel = lax.optimization_barrier(kernel)
    balance = (items * groups) / (codes * depth)
    weights_rows = None
    for sweep in range(ITERS):
        scaled = kernel.astype(jnp.float32)
        if weights_rows is not None:
            scaled = scaled * weights_rows[None, :, None]
        column_part = lax.optimization_barrier(jnp.sum(scaled, axis=1))
        column_parts = spread(column_part.astype(jnp.bfloat16), ITEM_AXES)
        column_total = jnp.sum(column_parts.astype(jnp.float32), axis=0)
        weights_cols = balance / column_total
        row_part = jnp.sum(
            kernel.astype(jnp.float32) * weights_cols[:, None, :], axis=(0, 2)
        )
        if sweep < ITERS - 1:
            row_part = lax.optimization_barrier(row_part).astype(jnp.bfloat16)
            row_parts = spread(row_part.reshape(-1, width), "z")
            row_total = jnp.sum(row_parts.astype(jnp.float32), axis=0)
            weights_rows = 1.0 / row_total.reshape(items)

    size = rows * depth
    mine = kernel[:, :size].astype(jnp.float32) * weights_cols[:, None, :]
    products = jnp.einsum(
        "pnk,pkd->nd", mine.astype(jnp.bfloat16), codebook, preferred_element_type=jnp.float32
    )
    products = products.astype(jnp.bfloat16).reshape(depth, rows, width)
    terms = jnp.concatenate([t.reshape(-1, width) for t in two_terms(row_part)])
    extra = terms.shape[0]
    terms = jnp.pad(terms, ((0, -extra % 8), (0, 0)))
    terms = jnp.broadcast_to(terms[None], (depth,) + terms.shape)
    packed = jnp.concatenate([products, terms], axis=1)
    packed, weights_cols = lax.optimization_barrier((packed, weights_cols[0]))
    packed = lax.all_to_all(packed, "z", 0, 0, tiled=True)
    total = jnp.sum(packed.astype(jnp.float32), axis=0)
    middle = rows + extra // 2
    row_total = total[rows:middle] + total[middle : rows + extra]
    weights_rows = 1.0 / row_total.reshape(items)

    again, weights_rows = lax.optimization_barrier((gathered, weights_rows))
    own_kernel = kernel_of(again, codebook[0], own_scale)
    transport = (own_kernel * weights_rows[:, None] * weights_cols[None, :]).astype(jnp.bfloat16)
    numerator = lax.dot_general(
        transport, gathered, (((0,), (0,)), ((), ())), preferred_element_type=jnp.float32
    )
    mass = jnp.sum(transport.astype(jnp.float32), axis=0)
    masses = jnp.stack([t.reshape(groups, share) for t in two_terms(mass)], axis=1)
    masses = jnp.pad(masses, ((0, 0), (0, 6), (0, width - share)))
    packed = jnp.concatenate(
        [numerator.astype(jnp.bfloat16).reshape(groups, share, width), masses], axis=1
    )
    packed = lax.all_to_all(packed, ITEM_AXES, 0, 0, tiled=True)

    own = lax.dynamic_slice_in_dim(weights_rows, own_at, rows)
    following = residuals.astype(jnp.float32) - total[:rows] * own[:, None]

    total = jnp.sum(packed.astype(jnp.float32), axis=0)
    mass_total = total[share, :share] + total[share + 1, :share]
    means = total[:share] / mass_total[:, None]
    new_codebook = spread(means.astype(MEANS), ("h", "l")).reshape(-1, width)
    new_codebook = new_codebook.astype(jnp.float32)
    return (new_codebook, following)


def solution(mesh):
    fine = Mesh(mesh.devices.reshape(4, 2, 4, 8, 2), ("h", "l", "x", "z", "c"))
    return jax.shard_map(
        shards,
        mesh=fine,
        in_specs=(P(("h", "l", "x", "z", "c"), None), P(("x", "z", "c"), None)),
        out_specs=(P(("x", "z", "c"), None), P(("h", "l", "x", "z", "c"), None)),
        check_vma=False,
    )
```
